32 devices in a mesh: layer: 4 (over y, core), row: 4 (over z), col: 2 (over x).
Axes of the slice: x: 2, y: 2, z: 4, core: 2. Of those that a mesh axis runs over, the one named last changes fastest.
Arguments:
- edge_weight: bfloat16 [2048, 2048], P('row', 'col'), may hold values from 0 to 1, as said below
Outputs:
- clustering: float32 [4, 512], P('row', ('layer', 'col'))
The draws below stay inside these ranges and needn't reach their ends.
Inputs may be any that keep to these rules, and one draw needn't show every extreme that they name: `edge_weight`: symmetric with a zero diagonal; every vertex v is linked to v - 1 and v + 1 (modulo 2048); an edge's entry lies in [0.2, 1], all other entries are 0.
All inputs are finite; a program needn't handle non-finite values.
Results may differ from the reference program's by a relative error of at most 0.0003.
Values may be sent and summed in bfloat16 or wider, within the bound.
A program may use at most 64 MiB of HBM per device.

```python
import jax
import jax.numpy as jnp
from jax import lax

VERTS = 2048
N_ROW = 4


def draw_edge_weight(key, part):
    keys = jax.random.split(jax.random.fold_in(key, 7), 4)
    index = jnp.arange(VERTS, dtype=jnp.float32)
    leaning = 0.25 * 4.0 ** (index / VERTS) * jax.random.uniform(keys[0], (VERTS,), minval=0.6, maxval=1.25)
    place = jax.random.uniform(keys[3], (VERTS,), minval=0.0, maxval=2.0 * jnp.pi)
    nearness = 0.5 + 0.5 * jnp.cos(place[:, None] - place[None, :])
    chance = jnp.sqrt(leaning[:, None] * leaning[None, :]) * (0.1 + 1.8 * nearness ** 4)
    coins = jax.random.uniform(keys[1], (VERTS, VERTS))
    first = jnp.arange(VERTS)[:, None]
    second = jnp.arange(VERTS)[None, :]
    upper = second > first
    linked = jnp.logical_and(coins < chance, upper)
    linked = jnp.logical_or(linked, linked.T)
    distance = jnp.abs(first - second)
    linked = jnp.logical_or(linked, jnp.logical_or(distance == 1, distance == VERTS - 1))
    values = jnp.exp(jax.random.uniform(keys[2], (VERTS, VERTS), minval=jnp.log(0.2), maxval=0.0))
    values = jnp.where(upper, values, 0.0)
    values = values + values.T
    return jnp.where(linked, values, 0.0).astype(jnp.float32).astype(jnp.bfloat16)


def setup_inputs(seed: int = 0) -> dict:
    arg_keys = jax.random.split(jax.random.key(seed), 2)
    edge_weight = draw_edge_weight(jax.random.fold_in(arg_keys[1], 71), 0)
    return {"edge_weight": edge_weight}


def reference(edge_weight):
    weights = edge_weight.astype(jnp.float32)
    order = jnp.arange(VERTS, dtype=jnp.int32)
    lower = jnp.where(order[:, None] > order[None, :], weights, jnp.zeros_like(weights))
    degree = jnp.sum(jnp.where(lower > 0, 1.0, 0.0).astype(jnp.float32), axis=1)
    span = VERTS // N_ROW

    def block_rows(index):
        rows = lax.dynamic_slice_in_dim(lower, index * span, span, 0)
        paths = jnp.dot(rows, lower, precision=lax.Precision.HIGHEST)
        return jnp.sum(paths * rows, axis=1)

    triangles = lax.map(block_rows, jnp.arange(N_ROW, dtype=jnp.int32)).reshape(VERTS)
    clustering = 2.0 * triangles / jnp.maximum(degree * (degree - 1.0), 2.0)
    return clustering.reshape(N_ROW, span)
```

```python
import functools

import jax
import jax.numpy as jnp
from jax import lax
from jax.experimental import pallas as pl
from jax.experimental.pallas import tpu as pltpu
from jax.sharding import PartitionSpec as P

STRIPE = 128
MESH = pl.DeviceIdType.MESH


def at(layer, row, col):
    return {"layer": layer, "row": row, "col": col}


def kernel(
    layers, rows, cols, w_ref, out_ref,
    block, mask_block, side, across, left, right, stage, cross_stage, column_sum, inbox,
    load_sem, keep_side_sem, keep_across_sem, keep_inbox_sem, side_send, side_recv,
    across_send, across_recv, plane_send, cross_send, inbox_recv,
):
    span = rows // cols
    m, n = w_ref.shape
    q = m // layers
    layer, row, col = (lax.axis_index(a) for a in ("layer", "row", "col"))
    group = row // span
    place = row % span
    above = col > group

    barrier = pltpu.get_barrier_semaphore()

    def greet(l, r, c):
        pl.semaphore_signal(barrier, inc=1, device_id=at(l, r, c), device_id_type=MESH)

    for l in range(layers):
        for c in range(cols):
            @pl.when(jnp.logical_or(l != layer, c != col))
            def _():
                greet(l, row, c)
    for s in range(span):
        @pl.when(s != place)
        def _():
            greet(layer, group * span + s, col)

    @pl.when(above)
    def _():
        for s in range(span):
            for l in range(layers):
                for c in range(cols):
                    greet(l, col * span + s, c)
    for r in range(rows):
        @pl.when(r < group * span)
        def _():
            for l in range(layers):
                greet(l, r, group)

    load = pltpu.make_async_copy(w_ref, block, load_sem)
    load.start()

    def side_source(s):
        return w_ref.at[:, pl.ds(pl.multiple_of(s * m + layer * q, q), q)]

    def side_slot(s):
        return side.at[:, pl.ds(s * q, q)]

    def across_slot(s):
        return across.at[pl.ds(pl.multiple_of(s * q, q), q), :]

    across_source = w_ref.at[pl.ds(pl.multiple_of(layer * q, q), q), :]
    keep_across = pltpu.make_async_copy(across_source, across_slot(place), keep_across_sem)
    keep_across.start()

    def keep_side(s):
        return pltpu.make_async_copy(side_source(s), side_slot(s), keep_side_sem.at[s])

    for s in range(span):
        @pl.when(s > place)
        def _():
            side[:, s * q:(s + 1) * q] = jnp.zeros((m, q), side.dtype)
            across[s * q:(s + 1) * q, :] = jnp.zeros((q, n), across.dtype)

        @pl.when(jnp.logical_and(col == group, s <= place))
        def _():
            keep_side(s).start()

    everyone = layers * cols - 1 + span - 1 + group * span * layers
    pl.semaphore_wait(barrier, everyone + jnp.where(above, span * layers * cols, 0))

    def side_copy(s, c):
        return pltpu.make_async_remote_copy(
            src_ref=side_source(s), dst_ref=side_slot(s), send_sem=side_send.at[s, c], recv_sem=side_recv.at[s],
            device_id=at(layer, row, c), device_id_type=MESH)

    def across_copy(s):
        return pltpu.make_async_remote_copy(
            src_ref=across_source, dst_ref=across_slot(place), send_sem=across_send.at[s],
            recv_sem=across_recv.at[place], device_id=at(layer, group * span + s, col), device_id_type=MESH)

    def side_sends(act):
        for s in range(span):
            for c in range(cols):
                @pl.when(jnp.logical_and(jnp.logical_and(col == group, c != col), s <= place))
                def _():
                    act(side_copy(s, c))

    def across_sends(act):
        for s in range(span):
            @pl.when(s > place)
            def _():
                act(across_copy(s))

    across_sends(lambda copy: copy.start())
    side_sends(lambda copy: copy.start())

    load.wait()
    per_layer = n // layers
    row_here = row * m + lax.broadcasted_iota(jnp.int32, (q, 1), 0)
    col_here = col * n + lax.broadcasted_iota(jnp.int32, (1, n), 1)
    for k in range(layers):
        held = block[k * q:(k + 1) * q, :].astype(jnp.float32)
        lower = row_here + k * q > col_here
        mask_block[k * q:(k + 1) * q, :] = jnp.where(jnp.logical_or(lower, above), held, 0.0)
        mine = col_here // per_layer == col * layers + layer
        linked = jnp.where(jnp.logical_and(jnp.logical_and(lower, held > 0), mine), 1.0, 0.0)
        counts = sum(linked[:, t:t + q] for t in range(0, n, q))
        stage[k, 1:2, :] = jnp.sum(counts.T, axis=0, keepdims=True)

    keep_across.wait()
    for s in range(span):
        @pl.when(jnp.logical_and(col == group, s <= place))
        def _():
            keep_side(s).wait()

        @pl.when(jnp.logical_and(col != group, s <= place))
        def _():
            side_copy(s, 0).wait_recv()
        inner = (group * span + s) * m + layer * q
        outer_rows = row * m + lax.broadcasted_iota(jnp.int32, (m, 1), 0)
        inner_cols = inner + lax.broadcasted_iota(jnp.int32, (1, q), 1)
        held = side[:, s * q:(s + 1) * q].astype(jnp.float32)
        left[:, s * q:(s + 1) * q] = jnp.where(outer_rows > inner_cols, held, 0.0).astype(left.dtype)
    for s in range(span):
        @pl.when(s < place)
        def _():
            pltpu.make_async_remote_copy(
                src_ref=across_source, dst_ref=across_slot(s), send_sem=across_send.at[s],
                recv_sem=across_recv.at[s], device_id=at(layer, row, col), device_id_type=MESH).wait_recv()
        inner_rows = (group * span + s) * m + layer * q + lax.broadcasted_iota(jnp.int32, (q, 1), 0)
        held = across[s * q:(s + 1) * q, :].astype(jnp.float32)
        right[s * q:(s + 1) * q, :] = jnp.where(
            jnp.logical_or(inner_rows > col_here, above), held, 0.0).astype(right.dtype)

    def products(k):
        paths = jnp.dot(left[k * q:(k + 1) * q, :], right[...], preferred_element_type=jnp.float32)
        return paths * mask_block[k * q:(k + 1) * q, :]

    in_plane = lambda l, c: pltpu.make_async_remote_copy(
        src_ref=stage.at[l], dst_ref=inbox.at[layer * cols + col], send_sem=plane_send.at[l, c],
        recv_sem=inbox_recv.at[layer * cols + col], device_id=at(l, row, c), device_id_type=MESH)
    to_self = pltpu.make_async_copy(stage.at[layer], inbox.at[layer * cols + col], keep_inbox_sem)

    def plane_sends(act, self_act):
        for l in range(layers):
            for c in range(cols):
                here = jnp.logical_and(l == layer, c == col)

                @pl.when(jnp.logical_not(here))
                def _():
                    act(in_plane(l, c))

                @pl.when(here)
                def _():
                    self_act(to_self)

    cross_slot = layers * cols + row * layers + layer
    cross = lambda s, l, c: pltpu.make_async_remote_copy(
        src_ref=cross_stage.at[s * layers + l], dst_ref=inbox.at[cross_slot],
        send_sem=cross_send.at[s * layers + l, c], recv_sem=inbox_recv.at[cross_slot],
        device_id=at(l, col * span + s, c), device_id_type=MESH)

    def cross_sends(act):
        for s in range(span):
            for l in range(layers):
                for c in range(cols):
                    act(cross(s, l, c))

    @pl.when(above)
    def _():
        total = jnp.zeros((1, n), jnp.float32)
        for k in range(layers):
            total = total + jnp.sum(products(k), axis=0, keepdims=True)
        for t in range(span * layers):
            cross_stage[t, 0:1, :] = total[:, t * q:(t + 1) * q]
            cross_stage[t, 1:2, :] = jnp.zeros((1, q), jnp.float32)
        cross_sends(lambda copy: copy.start())

    @pl.when(jnp.logical_not(above))
    def _():
        for k in range(layers):
            part = products(k)
            sums = sum(part[:, t:t + q] for t in range(0, n, q))
            stage[k, 0:1, :] = jnp.sum(sums.T, axis=0, keepdims=True)
        plane_sends(lambda copy: copy.start(), lambda copy: copy.start())

    column_sum[...] = jnp.zeros_like(column_sum)

    def take(slot):
        pltpu.make_async_remote_copy(
            src_ref=stage.at[0], dst_ref=inbox.at[slot], send_sem=plane_send.at[0, 0], recv_sem=inbox_recv.at[slot],
            device_id=at(layer, row, col), device_id_type=MESH).wait_recv()
        column_sum[...] += inbox[slot]

    for l in range(layers):
        for c in range(cols):
            here = jnp.logical_and(l == layer, c == col)

            @pl.when(jnp.logical_and(here, jnp.logical_not(above)))
            def _():
                to_self.wait()
                column_sum[...] += inbox[l * cols + c]

            @pl.when(jnp.logical_and(jnp.logical_not(here), c <= group))
            def _():
                take(l * cols + c)
    for r in range(rows):
        @pl.when(r < group * span)
        def _():
            for l in range(layers):
                take(layers * cols + r * layers + l)

    share = q // cols
    mine = jnp.zeros((2, share), jnp.float32)
    for c in range(cols):
        mine = jnp.where(c == col, column_sum[:, c * share:(c + 1) * share], mine)
    out_ref[...] = mine

    across_sends(lambda copy: copy.wait_send())
    side_sends(lambda copy: copy.wait_send())

    @pl.when(above)
    def _():
        cross_sends(lambda copy: copy.wait_send())

    @pl.when(jnp.logical_not(above))
    def _():
        plane_sends(lambda copy: copy.wait_send(), lambda copy: None)


def two_blocks(edge_weight):
    layers, rows, cols = (lax.axis_size(a) for a in ("layer", "row", "col"))
    m, n = edge_weight.shape
    q, span = m // layers, rows // cols
    slots = layers * cols + rows * layers
    dma = pltpu.SemaphoreType.DMA
    kind = edge_weight.dtype
    return pl.pallas_call(
        functools.partial(kernel, layers, rows, cols),
        out_shape=jax.ShapeDtypeStruct((2, q // cols), jnp.float32),
        in_specs=[pl.BlockSpec(memory_space=pl.ANY)],
        out_specs=pl.BlockSpec(memory_space=pltpu.VMEM),
        scratch_shapes=[
            pltpu.VMEM((m, n), kind),
            pltpu.VMEM((m, n), jnp.float32),
            pltpu.VMEM((m, span * q), kind),
            pltpu.VMEM((span * q, n), kind),
            pltpu.VMEM((m, span * q), kind),
            pltpu.VMEM((span * q, n), kind),
            pltpu.VMEM((layers, 2, q), jnp.float32),
            pltpu.VMEM((span * layers, 2, q), jnp.float32),
            pltpu.VMEM((2, q), jnp.float32),
            pltpu.VMEM((slots, 2, q), jnp.float32),
            dma, dma((span,)), dma, dma, dma((span, cols)), dma((span,)),
            dma((span,)), dma((span,)), dma((layers, cols)), dma((span * layers, cols)), dma((slots,)),
        ],
        compiler_params=pltpu.CompilerParams(collective_id=0, has_side_effects=True),
    )(edge_weight)


def three_blocks(edge_weight):
    layers, layer_index = lax.axis_size("layer"), lax.axis_index("layer")
    row_count, col_count = edge_weight.shape
    row_block = (lax.axis_index("row") * row_count + jnp.arange(row_count, dtype=jnp.int32)) // col_count
    lower = jnp.where(row_block[:, None] > lax.axis_index("col"), edge_weight, jnp.zeros_like(edge_weight))
    column_groups = lower.reshape(row_count, col_count // (STRIPE * layers), layers, STRIPE)
    left_local = lax.dynamic_index_in_dim(column_groups, layer_index, 2, keepdims=False).reshape(
        row_count, col_count // layers
    )
    row_groups = lower.reshape(row_count // (STRIPE * layers), layers, STRIPE, col_count)
    right_local = lax.dynamic_index_in_dim(row_groups, layer_index, 1, keepdims=False).reshape(
        row_count // layers, col_count
    )
    left_whole = lax.all_gather(left_local, "col", axis=1, tiled=True)
    right_whole = lax.all_gather(right_local, "row", axis=0, tiled=True)
    paths = jnp.dot(left_whole, right_whole, preferred_element_type=jnp.float32)
    triangles = jnp.sum(paths * lower, axis=1)
    layer_share = lax.psum_scatter(triangles, "layer", scatter_dimension=0, tiled=True)
    return lax.psum_scatter(layer_share, "col", scatter_dimension=0, tiled=True)


def local(edge_weight):
    sums = two_blocks(edge_weight)
    triangles, degree = sums[0], sums[1]
    if lax.axis_size("col") > 2:
        triangles = triangles + three_blocks(edge_weight)
    clustering = 2.0 * triangles / jnp.maximum(degree * (degree - 1.0), 2.0)
    return clustering.reshape(1, -1)


def solution(mesh):
    placed = (P("row", "col"),)
    return jax.shard_map(
        local, mesh=mesh, in_specs=placed, out_specs=P("row", ("layer", "col")), check_vma=False
    )
```

```python
import functools

import jax
import jax.numpy as jnp
from jax import lax
from jax.experimental import pallas as pl
from jax.experimental.pallas import tpu as pltpu
from jax.sharding import PartitionSpec as P

STRIPE = 128
CHUNKS = 4
MESH = pl.DeviceIdType.MESH


def at(layer, row, col):
    return {"layer": layer, "row": row, "col": col}


def kernel(
    layers, rows, cols, finish, w_ref, out_ref,
    block, side, across, sums, stage, cross_stage, total, inbox,
    load_sem, keep_side_sem, keep_across_sem, keep_inbox_sem, side_send, side_recv,
    across_send, across_recv, plane_send, cross_send, inbox_recv, plane_in, above_in,
):
    span = rows // cols
    m, n = w_ref.shape
    q = m // layers
    chunk = n // CHUNKS
    layer, row, col = (lax.axis_index(a) for a in ("layer", "row", "col"))
    group = row // span
    place = row % span
    above = col > group
    diagonal = col == group
    share = jnp.where(layer % 2 == 0, layer // 2, layers - 1 - layer // 2)

    load = pltpu.make_async_copy(w_ref, block, load_sem)
    load.start()

    barrier = pltpu.get_barrier_semaphore()

    def greet(l, r, c, semaphore=barrier):
        pl.semaphore_signal(semaphore, inc=1, device_id=at(l, r, c), device_id_type=MESH)

    near = layers - 1 + cols - 1
    for c in range(cols):
        @pl.when(c != col)
        def _():
            greet(layer, row, c)
    for r in range(rows):
        is_near = jnp.logical_and(
            r != row, jnp.logical_or(r // span == group, jnp.logical_or(r == row - 1, r == row + 1)))
        near = near + jnp.where(is_near, 1, 0)

        @pl.when(is_near)
        def _():
            greet(layer, r, col)
    for l in range(layers):
        @pl.when(l != layer)
        def _():
            greet(l, row, col)

    def side_source(s, first=0):
        start = pl.multiple_of(s * m + share * q, q)
        return w_ref.at[first * q:m, pl.ds(start, q)]

    def side_slot(s, first=0):
        return side.at[first * q:m, s * q:(s + 1) * q]

    def across_source(t):
        return w_ref.at[pl.ds(pl.multiple_of(share * q, q), q), t * chunk:(t + 1) * chunk]

    def across_slot(s, t):
        return across.at[pl.ds(pl.multiple_of(s * q, q), q), t * chunk:(t + 1) * chunk]

    keep_across = pltpu.make_async_copy(
        w_ref.at[pl.ds(pl.multiple_of(share * q, q), q), :],
        across.at[pl.ds(pl.multiple_of(place * q, q), q), :], keep_across_sem)
    keep_across.start()

    def keep_side(s):
        return pltpu.make_async_copy(side_source(s), side_slot(s), keep_side_sem.at[s])

    for s in range(span):
        @pl.when(s > place)
        def _():
            side[:, s * q:(s + 1) * q] = jnp.zeros((m, q), side.dtype)
            across[s * q:(s + 1) * q, :] = jnp.zeros((q, n), across.dtype)

        @pl.when(jnp.logical_and(diagonal, s <= place))
        def _():
            keep_side(s).start()

    pl.semaphore_wait(barrier, near)

    def side_copy(s, c, first):
        return pltpu.make_async_remote_copy(
            src_ref=side_source(s, first), dst_ref=side_slot(s, first), send_sem=side_send.at[s, c],
            recv_sem=side_recv.at[s], device_id=at(layer, row, c), device_id_type=MESH)

    def side_each(s, c, act):
        @pl.when(s < place)
        def _():
            act(side_copy(s, c, 0))
        for first in range(layers):
            @pl.when(jnp.logical_and(s == place, share == first))
            def _():
                act(side_copy(s, c, first))

    def side_sends(act):
        for s in range(span):
            for c in range(cols):
                @pl.when(jnp.logical_and(diagonal, c != col))
                def _():
                    side_each(s, c, act)

    def across_copy(s, t, origin):
        return pltpu.make_async_remote_copy(
            src_ref=across_source(t), dst_ref=across_slot(origin, t), send_sem=across_send.at[s, t],
            recv_sem=across_recv.at[origin, t], device_id=at(layer, group * span + s, col), device_id_type=MESH)

    def has_entries(origin, t):
        return jnp.logical_or(jnp.logical_not(diagonal), t * chunk < (origin + 1) * m)

    def across_sends(act):
        for t in range(CHUNKS):
            for s in range(span):
                @pl.when(jnp.logical_and(s > place, has_entries(place, t)))
                def _():
                    act(across_copy(s, t, place))

    across_sends(lambda copy: copy.start())
    side_sends(lambda copy: copy.start())

    for c in range(cols):
        @pl.when(c != col)
        def _():
            greet(layer, row, c, plane_in)

    load.wait()
    per_layer = n // layers
    row_here = row * m + lax.broadcasted_iota(jnp.int32, (q, 1), 0)
    col_here = col * n + lax.broadcasted_iota(jnp.int32, (1, n), 1)

    @pl.when(diagonal)
    def _():
        for k in range(layers):
            held = block[k * q:(k + 1) * q, :].astype(jnp.float32)
            block[k * q:(k + 1) * q, :] = jnp.where(row_here + k * q > col_here, held, 0.0).astype(block.dtype)

    @pl.when(jnp.logical_not(above))
    def _():
        mine = pl.ds(pl.multiple_of(layer * per_layer, per_layer), per_layer)
        for k in range(layers):
            linked = jnp.where(block[k * q:(k + 1) * q, mine].astype(jnp.float32) > 0, 1.0, 0.0)
            counts = sum(linked[:, t:t + q] for t in range(0, per_layer, q))
            stage[k, 1:2, :] = jnp.sum(counts.T, axis=0, keepdims=True)

    pl.semaphore_wait(plane_in, cols - 1)

    @pl.when(row < rows - 1)
    def _():
        pl.semaphore_wait(above_in, 1)

    @pl.when(row > 0)
    def _():
        greet(layer, row - 1, col, above_in)

    keep_across.wait()
    for s in range(span):
        @pl.when(jnp.logical_and(diagonal, s <= place))
        def _():
            keep_side(s).wait()

        @pl.when(jnp.logical_not(diagonal))
        def _():
            side_each(s, 0, lambda copy: copy.wait_recv())

        @pl.when(s == place)
        def _():
            inner = row * m + share * q + lax.broadcasted_iota(jnp.int32, (1, q), 1)
            outer = row * m + lax.broadcasted_iota(jnp.int32, (m, 1), 0)
            held = side[:, s * q:(s + 1) * q].astype(jnp.float32)
            side[:, s * q:(s + 1) * q] = jnp.where(outer > inner, held, 0.0).astype(side.dtype)

    def operand(t):
        for s in range(span):
            @pl.when(jnp.logical_and(s < place, has_entries(s, t)))
            def _():
                across_copy(0, t, s).wait_recv()

            @pl.when(diagonal)
            def _():
                inner = (group * span + s) * m + share * q + lax.broadcasted_iota(jnp.int32, (q, 1), 0)
                outer = col * n + t * chunk + lax.broadcasted_iota(jnp.int32, (1, chunk), 1)
                held = across[s * q:(s + 1) * q, t * chunk:(t + 1) * chunk].astype(jnp.float32)
                across[s * q:(s + 1) * q, t * chunk:(t + 1) * chunk] = jnp.where(
                    inner > outer, held, 0.0).astype(across.dtype)

    def products(k, t):
        here = slice(t * chunk, (t + 1) * chunk)
        paths = jnp.dot(side[k * q:(k + 1) * q, :], across[:, here], preferred_element_type=jnp.float32)
        return paths * block[k * q:(k + 1) * q, here].astype(jnp.float32)

    in_plane = lambda l, c: pltpu.make_async_remote_copy(
        src_ref=stage.at[l], dst_ref=inbox.at[layer * cols + col], send_sem=plane_send.at[l, c],
        recv_sem=inbox_recv.at[layer * cols + col], device_id=at(l, row, c), device_id_type=MESH)
    to_self = pltpu.make_async_copy(stage.at[layer], inbox.at[layer * cols + col], keep_inbox_sem)

    def plane_sends(act, self_act):
        for l in range(layers):
            for c in range(cols):
                here = jnp.logical_and(l == layer, c == col)

                @pl.when(jnp.logical_not(here))
                def _():
                    act(in_plane(l, c))

                @pl.when(here)
                def _():
                    self_act(to_self)

    cross_slot = layers * cols + row * layers + layer
    cross = lambda s, l, c: pltpu.make_async_remote_copy(
        src_ref=cross_stage.at[s * layers + l], dst_ref=inbox.at[cross_slot],
        send_sem=cross_send.at[s * layers + l, c], recv_sem=inbox_recv.at[cross_slot],
        device_id=at(l, col * span + s, c), device_id_type=MESH)

    def cross_sends(act):
        for s in reversed(range(span)):
            for l in range(layers):
                for c in range(cols):
                    act(cross(s, l, c))

    @pl.when(above)
    def _():
        for t in range(CHUNKS):
            operand(t)
            part = sum(jnp.sum(products(k, t), axis=0, keepdims=True) for k in range(layers))
            for u in range(0, chunk, q):
                v = (t * chunk + u) // q
                cross_stage[v, 0:1, :] = part[:, u:u + q]
                cross_stage[v, 1:2, :] = jnp.zeros((1, q), jnp.float32)
        cross_sends(lambda copy: copy.start())

    @pl.when(jnp.logical_not(above))
    def _():
        for t in range(CHUNKS):
            operand(t)
            for k in range(layers):
                part = products(k, t)
                part = sum(part[:, u:u + q] for u in range(0, chunk, q))
                sums[k] = part if t == 0 else sums[k] + part
        for k in range(layers):
            stage[k, 0:1, :] = jnp.sum(sums[k].T, axis=0, keepdims=True)
        plane_sends(lambda copy: copy.start(), lambda copy: copy.start())

    total[...] = jnp.zeros_like(total)

    def take(slot):
        pltpu.make_async_remote_copy(
            src_ref=stage.at[0], dst_ref=inbox.at[slot], send_sem=plane_send.at[0, 0], recv_sem=inbox_recv.at[slot],
            device_id=at(layer, row, col), device_id_type=MESH).wait_recv()
        total[...] += inbox[slot]

    for l in range(layers):
        for c in range(cols):
            here = jnp.logical_and(l == layer, c == col)

            @pl.when(jnp.logical_and(here, jnp.logical_not(above)))
            def _():
                to_self.wait()
                total[...] += inbox[l * cols + c]

            @pl.when(jnp.logical_and(jnp.logical_not(here), c <= group))
            def _():
                take(l * cols + c)
    for r in range(rows):
        @pl.when(r < group * span)
        def _():
            for l in range(layers):
                take(layers * cols + r * layers + l)

    part = q // cols
    mine = jnp.zeros((2, part), jnp.float32)
    for c in range(cols):
        mine = jnp.where(c == col, total[:, c * part:(c + 1) * part], mine)
    out_ref[...] = clustering_of(mine[0:1], mine[1:2]) if finish else mine

    across_sends(lambda copy: copy.wait_send())
    side_sends(lambda copy: copy.wait_send())

    @pl.when(above)
    def _():
        cross_sends(lambda copy: copy.wait_send())

    @pl.when(jnp.logical_not(above))
    def _():
        plane_sends(lambda copy: copy.wait_send(), lambda copy: None)


def clustering_of(triangles, degree):
    return 2.0 * triangles / jnp.maximum(degree * (degree - 1.0), 2.0)


def two_blocks(edge_weight, finish):
    layers, rows, cols = (lax.axis_size(a) for a in ("layer", "row", "col"))
    m, n = edge_weight.shape
    q, span = m // layers, rows // cols
    slots = layers * cols + rows * layers
    dma, flag = pltpu.SemaphoreType.DMA, pltpu.SemaphoreType.REGULAR
    kind = edge_weight.dtype
    return pl.pallas_call(
        functools.partial(kernel, layers, rows, cols, finish),
        out_shape=jax.ShapeDtypeStruct((1 if finish else 2, q // cols), jnp.float32),
        in_specs=[pl.BlockSpec(memory_space=pl.ANY)],
        out_specs=pl.BlockSpec(memory_space=pltpu.VMEM),
        scratch_shapes=[
            pltpu.VMEM((m, n), kind),
            pltpu.VMEM((m, span * q), kind),
            pltpu.VMEM((span * q, n), kind),
            pltpu.VMEM((layers, q, q), jnp.float32),
            pltpu.VMEM((layers, 2, q), jnp.float32),
            pltpu.VMEM((span * layers, 2, q), jnp.float32),
            pltpu.VMEM((2, q), jnp.float32),
            pltpu.VMEM((slots, 2, q), jnp.float32),
            dma, dma((span,)), dma, dma, dma((span, cols)), dma((span,)),
            dma((span, CHUNKS)), dma((span, CHUNKS)), dma((layers, cols)), dma((span * layers, cols)), dma((slots,)),
            flag, flag,
        ],
        compiler_params=pltpu.CompilerParams(collective_id=0, has_side_effects=True),
    )(edge_weight)


def three_blocks(edge_weight):
    layers, layer_index = lax.axis_size("layer"), lax.axis_index("layer")
    row_count, col_count = edge_weight.shape
    row_block = (lax.axis_index("row") * row_count + jnp.arange(row_count, dtype=jnp.int32)) // col_count
    lower = jnp.where(row_block[:, None] > lax.axis_index("col"), edge_weight, jnp.zeros_like(edge_weight))
    column_groups = lower.reshape(row_count, col_count // (STRIPE * layers), layers, STRIPE)
    left_local = lax.dynamic_index_in_dim(column_groups, layer_index, 2, keepdims=False).reshape(
        row_count, col_count // layers
    )
    row_groups = lower.reshape(row_count // (STRIPE * layers), layers, STRIPE, col_count)
    right_local = lax.dynamic_index_in_dim(row_groups, layer_index, 1, keepdims=False).reshape(
        row_count // layers, col_count
    )
    left_whole = lax.all_gather(left_local, "col", axis=1, tiled=True)
    right_whole = lax.all_gather(right_local, "row", axis=0, tiled=True)
    paths = jnp.dot(left_whole, right_whole, preferred_element_type=jnp.float32)
    triangles = jnp.sum(paths * lower, axis=1)
    layer_share = lax.psum_scatter(triangles, "layer", scatter_dimension=0, tiled=True)
    return lax.psum_scatter(layer_share, "col", scatter_dimension=0, tiled=True)


def local(edge_weight):
    if lax.axis_size("col") == 2:
        return two_blocks(edge_weight, finish=True)
    triangles, degree = two_blocks(edge_weight, finish=False)
    return clustering_of(triangles + three_blocks(edge_weight), degree).reshape(1, -1)


def solution(mesh):
    placed = (P("row", "col"),)
    return jax.shard_map(
        local, mesh=mesh, in_specs=placed, out_specs=P("row", ("layer", "col")), check_vma=False
    )
```

```python
import functools

import jax
import jax.numpy as jnp
from jax import lax
from jax.experimental import pallas as pl
from jax.experimental.pallas import tpu as pltpu
from jax.sharding import PartitionSpec as P

STRIPE = 128
CHUNKS = 4
MESH = pl.DeviceIdType.MESH


def at(layer, row, col):
    return {"layer": layer, "row": row, "col": col}


def kernel(
    layers, rows, cols, finish, w_ref, out_ref,
    block, side, across, sums, stage, cross_stage, passed, total, inbox,
    load_sem, keep_side_sem, keep_across_sem, keep_inbox_sem, side_send, side_recv,
    across_send, across_recv, pass_send, pass_recv, plane_send, cross_send, inbox_recv, plane_in, above_in,
):
    span = rows // cols
    m, n = w_ref.shape
    q = m // layers
    chunk = n // CHUNKS
    layer, row, col = (lax.axis_index(a) for a in ("layer", "row", "col"))
    group = row // span
    place = row % span
    above = col > group
    diagonal = col == group
    share = jnp.where(layer % 2 == 0, layer // 2, layers - 1 - layer // 2)

    load = pltpu.make_async_copy(w_ref, block, load_sem)
    load.start()

    barrier = pltpu.get_barrier_semaphore()

    def greet(l, r, c, semaphore=barrier):
        pl.semaphore_signal(semaphore, inc=1, device_id=at(l, r, c), device_id_type=MESH)

    near = layers - 1 + cols - 1
    for c in range(cols):
        @pl.when(c != col)
        def _():
            greet(layer, row, c)
    for r in range(rows):
        is_near = jnp.logical_and(
            r != row, jnp.logical_or(r // span == group, jnp.logical_or(r == row - 1, r == row + 1)))
        near = near + jnp.where(is_near, 1, 0)

        @pl.when(is_near)
        def _():
            greet(layer, r, col)
    for l in range(layers):
        @pl.when(l != layer)
        def _():
            greet(l, row, col)

    def side_source(s, first=0):
        start = pl.multiple_of(s * m + share * q, q)
        return w_ref.at[first * q:m, pl.ds(start, q)]

    def side_slot(s, first=0):
        return side.at[first * q:m, s * q:(s + 1) * q]

    def across_source(t):
        return w_ref.at[pl.ds(pl.multiple_of(share * q, q), q), t * chunk:(t + 1) * chunk]

    def across_slot(s, t):
        return across.at[pl.ds(pl.multiple_of(s * q, q), q), t * chunk:(t + 1) * chunk]

    keep_across = pltpu.make_async_copy(
        w_ref.at[pl.ds(pl.multiple_of(share * q, q), q), :],
        across.at[pl.ds(pl.multiple_of(place * q, q), q), :], keep_across_sem)
    keep_across.start()

    def keep_side(s):
        return pltpu.make_async_copy(side_source(s), side_slot(s), keep_side_sem.at[s])

    for s in range(span):
        @pl.when(s > place)
        def _():
            side[:, s * q:(s + 1) * q] = jnp.zeros((m, q), side.dtype)
            across[s * q:(s + 1) * q, :] = jnp.zeros((q, n), across.dtype)

        @pl.when(jnp.logical_and(diagonal, s <= place))
        def _():
            keep_side(s).start()

    pl.semaphore_wait(barrier, near)

    def side_copy(s, c, first):
        return pltpu.make_async_remote_copy(
            src_ref=side_source(s, first), dst_ref=side_slot(s, first), send_sem=side_send.at[s, c],
            recv_sem=side_recv.at[s], device_id=at(layer, row, c), device_id_type=MESH)

    def side_each(s, c, act):
        @pl.when(s < place)
        def _():
            act(side_copy(s, c, 0))
        for first in range(layers):
            @pl.when(jnp.logical_and(s == place, share == first))
            def _():
                act(side_copy(s, c, first))

    def side_sends(act):
        for s in range(span):
            for c in range(cols):
                @pl.when(jnp.logical_and(diagonal, c != col))
                def _():
                    side_each(s, c, act)

    def across_copy(s, t, origin):
        return pltpu.make_async_remote_copy(
            src_ref=across_source(t), dst_ref=across_slot(origin, t), send_sem=across_send.at[s, t],
            recv_sem=across_recv.at[origin, t], device_id=at(layer, group * span + s, col), device_id_type=MESH)

    def has_entries(origin, t):
        return jnp.logical_or(jnp.logical_not(diagonal), t * chunk < (origin + 1) * m)

    def across_sends(act):
        for t in range(CHUNKS):
            for s in range(span):
                @pl.when(jnp.logical_and(s > place, has_entries(place, t)))
                def _():
                    act(across_copy(s, t, place))

    across_sends(lambda copy: copy.start())
    side_sends(lambda copy: copy.start())

    for c in range(cols):
        @pl.when(c != col)
        def _():
            greet(layer, row, c, plane_in)

    load.wait()
    per_layer = n // layers
    row_here = row * m + lax.broadcasted_iota(jnp.int32, (q, 1), 0)
    col_here = col * n + lax.broadcasted_iota(jnp.int32, (1, n), 1)

    @pl.when(diagonal)
    def _():
        for k in range(layers):
            held = block[k * q:(k + 1) * q, :].astype(jnp.float32)
            block[k * q:(k + 1) * q, :] = jnp.where(row_here + k * q > col_here, held, 0.0).astype(block.dtype)

    pl.semaphore_wait(plane_in, cols - 1)

    @pl.when(jnp.logical_and(row >= span - 1, row < rows - 1))
    def _():
        pl.semaphore_wait(above_in, 1)

    @pl.when(row > span - 1)
    def _():
        greet(layer, row - 1, col, above_in)

    @pl.when(jnp.logical_not(above))
    def _():
        mine = pl.ds(pl.multiple_of(layer * per_layer, per_layer), per_layer)
        for k in range(layers):
            linked = jnp.where(block[k * q:(k + 1) * q, mine].astype(jnp.float32) > 0, 1.0, 0.0)
            counts = sum(linked[:, t:t + q] for t in range(0, per_layer, q))
            stage[k, 1:2, :] = jnp.sum(counts.T, axis=0, keepdims=True)

    keep_across.wait()
    for s in range(span):
        @pl.when(jnp.logical_and(diagonal, s <= place))
        def _():
            keep_side(s).wait()

        @pl.when(jnp.logical_not(diagonal))
        def _():
            side_each(s, 0, lambda copy: copy.wait_recv())

        @pl.when(s == place)
        def _():
            inner = row * m + share * q + lax.broadcasted_iota(jnp.int32, (1, q), 1)
            outer = row * m + lax.broadcasted_iota(jnp.int32, (m, 1), 0)
            held = side[:, s * q:(s + 1) * q].astype(jnp.float32)
            side[:, s * q:(s + 1) * q] = jnp.where(outer > inner, held, 0.0).astype(side.dtype)

    def operand(t):
        for s in range(span):
            @pl.when(jnp.logical_and(s < place, has_entries(s, t)))
            def _():
                across_copy(0, t, s).wait_recv()

            @pl.when(diagonal)
            def _():
                inner = (group * span + s) * m + share * q + lax.broadcasted_iota(jnp.int32, (q, 1), 0)
                outer = col * n + t * chunk + lax.broadcasted_iota(jnp.int32, (1, chunk), 1)
                held = across[s * q:(s + 1) * q, t * chunk:(t + 1) * chunk].astype(jnp.float32)
                across[s * q:(s + 1) * q, t * chunk:(t + 1) * chunk] = jnp.where(
                    inner > outer, held, 0.0).astype(across.dtype)

    def products(k, t):
        here = slice(t * chunk, (t + 1) * chunk)
        paths = jnp.dot(side[k * q:(k + 1) * q, :], across[:, here], preferred_element_type=jnp.float32)
        return paths * block[k * q:(k + 1) * q, here].astype(jnp.float32)

    in_plane = lambda l, c: pltpu.make_async_remote_copy(
        src_ref=stage.at[l], dst_ref=inbox.at[layer * cols + col], send_sem=plane_send.at[l, c],
        recv_sem=inbox_recv.at[layer * cols + col], device_id=at(l, row, c), device_id_type=MESH)
    to_self = pltpu.make_async_copy(stage.at[layer], inbox.at[layer * cols + col], keep_inbox_sem)

    def plane_sends(act, self_act):
        for l in range(layers):
            for c in range(cols):
                here = jnp.logical_and(l == layer, c == col)

                @pl.when(jnp.logical_not(here))
                def _():
                    act(in_plane(l, c))

                @pl.when(here)
                def _():
                    self_act(to_self)

    onward = pltpu.make_async_remote_copy(
        src_ref=cross_stage, dst_ref=passed, send_sem=pass_send, recv_sem=pass_recv,
        device_id=at(layer, jnp.minimum(row + 1, rows - 1), col), device_id_type=MESH)
    cross_slot = layers * cols + group * layers + layer
    cross = lambda s, l, c: pltpu.make_async_remote_copy(
        src_ref=cross_stage.at[s * layers + l], dst_ref=inbox.at[cross_slot],
        send_sem=cross_send.at[s * layers + l, c], recv_sem=inbox_recv.at[cross_slot],
        device_id=at(l, col * span + s, c), device_id_type=MESH)

    def cross_sends(act):
        for s in reversed(range(span)):
            for l in range(layers):
                for c in range(cols):
                    act(cross(s, l, c))

    @pl.when(above)
    def _():
        for t in range(CHUNKS):
            operand(t)
            part = sum(jnp.sum(products(k, t), axis=0, keepdims=True) for k in range(layers))
            for u in range(0, chunk, q):
                v = (t * chunk + u) // q
                cross_stage[v, 0:1, :] = part[:, u:u + q]
                cross_stage[v, 1:2, :] = jnp.zeros((1, q), jnp.float32)

        @pl.when(place > 0)
        def _():
            onward.wait_recv()
            cross_stage[...] += passed[...]

        @pl.when(place < span - 1)
        def _():
            onward.start()

        @pl.when(place == span - 1)
        def _():
            cross_sends(lambda copy: copy.start())

    @pl.when(jnp.logical_not(above))
    def _():
        for t in range(CHUNKS):
            operand(t)
            for k in range(layers):
                part = products(k, t)
                part = sum(part[:, u:u + q] for u in range(0, chunk, q))
                sums[k] = part if t == 0 else sums[k] + part
        for k in range(layers):
            stage[k, 0:1, :] = jnp.sum(sums[k].T, axis=0, keepdims=True)
        plane_sends(lambda copy: copy.start(), lambda copy: copy.start())

    total[...] = jnp.zeros_like(total)

    def take(slot):
        pltpu.make_async_remote_copy(
            src_ref=stage.at[0], dst_ref=inbox.at[slot], send_sem=plane_send.at[0, 0], recv_sem=inbox_recv.at[slot],
            device_id=at(layer, row, col), device_id_type=MESH).wait_recv()
        total[...] += inbox[slot]

    for l in range(layers):
        for c in range(cols):
            here = jnp.logical_and(l == layer, c == col)

            @pl.when(jnp.logical_and(here, jnp.logical_not(above)))
            def _():
                to_self.wait()
                total[...] += inbox[l * cols + c]

            @pl.when(jnp.logical_and(jnp.logical_not(here), c <= group))
            def _():
                take(l * cols + c)
    for g in range(cols):
        @pl.when(g < group)
        def _():
            for l in range(layers):
                take(layers * cols + g * layers + l)

    part = q // cols
    mine = jnp.zeros((2, part), jnp.float32)
    for c in range(cols):
        mine = jnp.where(c == col, total[:, c * part:(c + 1) * part], mine)
    out_ref[...] = clustering_of(mine[0:1], mine[1:2]) if finish else mine

    across_sends(lambda copy: copy.wait_send())
    side_sends(lambda copy: copy.wait_send())

    @pl.when(jnp.logical_and(above, place < span - 1))
    def _():
        onward.wait_send()

    @pl.when(jnp.logical_and(above, place == span - 1))
    def _():
        cross_sends(lambda copy: copy.wait_send())

    @pl.when(jnp.logical_not(above))
    def _():
        plane_sends(lambda copy: copy.wait_send(), lambda copy: None)


def clustering_of(triangles, degree):
    return 2.0 * triangles / jnp.maximum(degree * (degree - 1.0), 2.0)


def two_blocks(edge_weight, finish):
    layers, rows, cols = (lax.axis_size(a) for a in ("layer", "row", "col"))
    m, n = edge_weight.shape
    q, span = m // layers, rows // cols
    slots = 2 * layers * cols
    dma, flag = pltpu.SemaphoreType.DMA, pltpu.SemaphoreType.REGULAR
    kind = edge_weight.dtype
    return pl.pallas_call(
        functools.partial(kernel, layers, rows, cols, finish),
        out_shape=jax.ShapeDtypeStruct((1 if finish else 2, q // cols), jnp.float32),
        in_specs=[pl.BlockSpec(memory_space=pl.ANY)],
        out_specs=pl.BlockSpec(memory_space=pltpu.VMEM),
        scratch_shapes=[
            pltpu.VMEM((m, n), kind),
            pltpu.VMEM((m, span * q), kind),
            pltpu.VMEM((span * q, n), kind),
            pltpu.VMEM((layers, q, q), jnp.float32),
            pltpu.VMEM((layers, 2, q), jnp.float32),
            pltpu.VMEM((span * layers, 2, q), jnp.float32),
            pltpu.VMEM((span * layers, 2, q), jnp.float32),
            pltpu.VMEM((2, q), jnp.float32),
            pltpu.VMEM((slots, 2, q), jnp.float32),
            dma, dma((span,)), dma, dma, dma((span, cols)), dma((span,)),
            dma((span, CHUNKS)), dma((span, CHUNKS)), dma, dma, dma((layers, cols)), dma((span * layers, cols)), dma((slots,)),
            flag, flag,
        ],
        compiler_params=pltpu.CompilerParams(collective_id=0, has_side_effects=True),
    )(edge_weight)


def three_blocks(edge_weight):
    layers, layer_index = lax.axis_size("layer"), lax.axis_index("layer")
    row_count, col_count = edge_weight.shape
    row_block = (lax.axis_index("row") * row_count + jnp.arange(row_count, dtype=jnp.int32)) // col_count
    lower = jnp.where(row_block[:, None] > lax.axis_index("col"), edge_weight, jnp.zeros_like(edge_weight))
    column_groups = lower.reshape(row_count, col_count // (STRIPE * layers), layers, STRIPE)
    left_local = lax.dynamic_index_in_dim(column_groups, layer_index, 2, keepdims=False).reshape(
        row_count, col_count // layers
    )
    row_groups = lower.reshape(row_count // (STRIPE * layers), layers, STRIPE, col_count)
    right_local = lax.dynamic_index_in_dim(row_groups, layer_index, 1, keepdims=False).reshape(
        row_count // layers, col_count
    )
    left_whole = lax.all_gather(left_local, "col", axis=1, tiled=True)
    right_whole = lax.all_gather(right_local, "row", axis=0, tiled=True)
    paths = jnp.dot(left_whole, right_whole, preferred_element_type=jnp.float32)
    triangles = jnp.sum(paths * lower, axis=1)
    layer_share = lax.psum_scatter(triangles, "layer", scatter_dimension=0, tiled=True)
    return lax.psum_scatter(layer_share, "col", scatter_dimension=0, tiled=True)


def local(edge_weight):
    if lax.axis_size("col") == 2:
        return two_blocks(edge_weight, finish=True)
    triangles, degree = two_blocks(edge_weight, finish=False)
    return clustering_of(triangles + three_blocks(edge_weight), degree).reshape(1, -1)


def solution(mesh):
    placed = (P("row", "col"),)
    return jax.shard_map(
        local, mesh=mesh, in_specs=placed, out_specs=P("row", ("layer", "col")), check_vma=False
    )
```

```python
import functools

import jax
import jax.numpy as jnp
from jax import lax
from jax.experimental import pallas as pl
from jax.experimental.pallas import tpu as pltpu
from jax.sharding import PartitionSpec as P

STRIPE = 128
MESH = pl.DeviceIdType.MESH


def at(layer, row, col):
    return {"layer": layer, "row": row, "col": col}


def kernel(
    layers, rows, cols, finish, w_ref, out_ref,
    block, side, across, sums, stage, cross_stage, passed, total, inbox,
    load_sem, keep_side_sem, keep_across_sem, keep_inbox_sem, side_send, side_recv,
    across_send, across_recv, pass_send, pass_recv, plane_send, cross_send, inbox_recv, plane_in, above_in,
):
    span = rows // cols
    m, n = w_ref.shape
    q = m // layers
    chunk = n // layers
    layer, row, col = (lax.axis_index(a) for a in ("layer", "row", "col"))
    group = row // span
    place = row % span
    above = col > group
    diagonal = col == group
    share = jnp.where(layer % 2 == 0, layer // 2, layers - 1 - layer // 2)

    load = pltpu.make_async_copy(w_ref, block, load_sem)
    load.start()

    barrier = pltpu.get_barrier_semaphore()

    def greet(l, r, c, semaphore=barrier):
        pl.semaphore_signal(semaphore, inc=1, device_id=at(l, r, c), device_id_type=MESH)

    near = layers - 1 + cols - 1
    for c in range(cols):
        @pl.when(c != col)
        def _():
            greet(layer, row, c)
    for r in range(rows):
        is_near = jnp.logical_and(
            r != row, jnp.logical_or(r // span == group, jnp.logical_or(r == row - 1, r == row + 1)))
        near = near + jnp.where(is_near, 1, 0)

        @pl.when(is_near)
        def _():
            greet(layer, r, col)
    for l in range(layers):
        @pl.when(l != layer)
        def _():
            greet(l, row, col)

    def side_source(s, k):
        return w_ref.at[k * q:(k + 1) * q, pl.ds(pl.multiple_of(s * m + share * q, q), q)]

    def side_slot(s, k):
        return side.at[k * q:(k + 1) * q, s * q:(s + 1) * q]

    def across_source(t):
        return w_ref.at[pl.ds(pl.multiple_of(share * q, q), q), t * chunk:(t + 1) * chunk]

    def across_slot(s, t):
        return across.at[pl.ds(pl.multiple_of(s * q, q), q), t * chunk:(t + 1) * chunk]

    keep_across = pltpu.make_async_copy(
        w_ref.at[pl.ds(pl.multiple_of(share * q, q), q), :],
        across.at[pl.ds(pl.multiple_of(place * q, q), q), :], keep_across_sem)
    keep_across.start()

    def keep_side(s):
        return pltpu.make_async_copy(
            w_ref.at[:, pl.ds(pl.multiple_of(s * m + share * q, q), q)], side.at[:, s * q:(s + 1) * q],
            keep_side_sem.at[s])

    for s in range(span):
        @pl.when(s > place)
        def _():
            side[:, s * q:(s + 1) * q] = jnp.zeros((m, q), side.dtype)
            across[s * q:(s + 1) * q, :] = jnp.zeros((q, n), across.dtype)

        @pl.when(jnp.logical_and(diagonal, s <= place))
        def _():
            keep_side(s).start()

    pl.semaphore_wait(barrier, near)

    def side_copy(s, k, c):
        return pltpu.make_async_remote_copy(
            src_ref=side_source(s, k), dst_ref=side_slot(s, k), send_sem=side_send.at[s, k, c],
            recv_sem=side_recv.at[s, k], device_id=at(layer, row, c), device_id_type=MESH)

    def side_has_entries(s, k):
        return jnp.logical_or(s < place, jnp.logical_and(s == place, k >= share))

    def side_sends(act):
        for k in range(layers):
            for s in range(span):
                for c in range(cols):
                    @pl.when(jnp.logical_and(jnp.logical_and(diagonal, c != col), side_has_entries(s, k)))
                    def _():
                        act(side_copy(s, k, c))

    def across_copy(s, t, origin):
        return pltpu.make_async_remote_copy(
            src_ref=across_source(t), dst_ref=across_slot(origin, t), send_sem=across_send.at[s, t],
            recv_sem=across_recv.at[origin, t], device_id=at(layer, group * span + s, col), device_id_type=MESH)

    def has_entries(origin, t):
        return jnp.logical_or(jnp.logical_not(diagonal), t * chunk < (origin + 1) * m)

    def across_sends(act):
        for t in range(layers):
            for s in range(span):
                @pl.when(jnp.logical_and(s > place, has_entries(place, t)))
                def _():
                    act(across_copy(s, t, place))

    across_sends(lambda copy: copy.start())
    side_sends(lambda copy: copy.start())

    for c in range(cols):
        @pl.when(c != col)
        def _():
            greet(layer, row, c, plane_in)

    load.wait()
    per_layer = n // layers
    row_here = row * m + lax.broadcasted_iota(jnp.int32, (q, 1), 0)
    col_here = col * n + lax.broadcasted_iota(jnp.int32, (1, n), 1)

    @pl.when(diagonal)
    def _():
        for k in range(layers):
            held = block[k * q:(k + 1) * q, :].astype(jnp.float32)
            block[k * q:(k + 1) * q, :] = jnp.where(row_here + k * q > col_here, held, 0.0).astype(block.dtype)

    pl.semaphore_wait(plane_in, cols - 1)

    @pl.when(jnp.logical_and(row >= span - 1, row < rows - 1))
    def _():
        pl.semaphore_wait(above_in, 1)

    @pl.when(row > span - 1)
    def _():
        greet(layer, row - 1, col, above_in)

    @pl.when(jnp.logical_not(above))
    def _():
        mine = pl.ds(pl.multiple_of(layer * per_layer, per_layer), per_layer)
        for k in range(layers):
            linked = jnp.where(block[k * q:(k + 1) * q, mine].astype(jnp.float32) > 0, 1.0, 0.0)
            counts = sum(linked[:, t:t + q] for t in range(0, per_layer, q))
            stage[k, 1:2, :] = jnp.sum(counts.T, axis=0, keepdims=True)

    keep_across.wait()
    for s in range(span):
        @pl.when(jnp.logical_and(diagonal, s <= place))
        def _():
            keep_side(s).wait()

    def side_operand(k):
        for s in range(span):
            @pl.when(jnp.logical_and(jnp.logical_not(diagonal), side_has_entries(s, k)))
            def _():
                side_copy(s, k, 0).wait_recv()

            @pl.when(s == place)
            def _():
                inner = row * m + share * q + lax.broadcasted_iota(jnp.int32, (1, q), 1)
                held = side[k * q:(k + 1) * q, s * q:(s + 1) * q].astype(jnp.float32)
                side[k * q:(k + 1) * q, s * q:(s + 1) * q] = jnp.where(
                    row_here + k * q > inner, held, 0.0).astype(side.dtype)

    def across_operand(t):
        for s in range(span):
            @pl.when(jnp.logical_and(s < place, has_entries(s, t)))
            def _():
                across_copy(0, t, s).wait_recv()

            @pl.when(diagonal)
            def _():
                inner = (group * span + s) * m + share * q + lax.broadcasted_iota(jnp.int32, (q, 1), 0)
                outer = col * n + t * chunk + lax.broadcasted_iota(jnp.int32, (1, chunk), 1)
                held = across[s * q:(s + 1) * q, t * chunk:(t + 1) * chunk].astype(jnp.float32)
                across[s * q:(s + 1) * q, t * chunk:(t + 1) * chunk] = jnp.where(
                    inner > outer, held, 0.0).astype(across.dtype)

    def products(k, t):
        here = slice(t * chunk, (t + 1) * chunk)
        paths = jnp.dot(side[k * q:(k + 1) * q, :], across[:, here], preferred_element_type=jnp.float32)
        return paths * block[k * q:(k + 1) * q, here].astype(jnp.float32)

    in_plane = lambda l, c: pltpu.make_async_remote_copy(
        src_ref=stage.at[l], dst_ref=inbox.at[layer * cols + col], send_sem=plane_send.at[l, c],
        recv_sem=inbox_recv.at[layer * cols + col], device_id=at(l, row, c), device_id_type=MESH)
    to_self = pltpu.make_async_copy(stage.at[layer], inbox.at[layer * cols + col], keep_inbox_sem)

    def plane_sends(act, self_act):
        for l in range(layers):
            for c in range(cols):
                here = jnp.logical_and(l == layer, c == col)

                @pl.when(jnp.logical_not(here))
                def _():
                    act(in_plane(l, c))

                @pl.when(here)
                def _():
                    self_act(to_self)

    onward = pltpu.make_async_remote_copy(
        src_ref=cross_stage, dst_ref=passed, send_sem=pass_send, recv_sem=pass_recv,
        device_id=at(layer, jnp.minimum(row + 1, rows - 1), col), device_id_type=MESH)
    cross_slot = layers * cols + group * layers + layer
    cross = lambda s, l, c: pltpu.make_async_remote_copy(
        src_ref=cross_stage.at[s * layers + l], dst_ref=inbox.at[cross_slot],
        send_sem=cross_send.at[s * layers + l, c], recv_sem=inbox_recv.at[cross_slot],
        device_id=at(l, col * span + s, c), device_id_type=MESH)

    def cross_sends(act):
        for s in reversed(range(span)):
            for l in range(layers):
                for c in range(cols):
                    act(cross(s, l, c))

    @pl.when(above)
    def _():
        cross_stage[...] = jnp.zeros_like(cross_stage)
        for shell in range(layers):
            side_operand(shell)
            across_operand(shell)
            for t in range(shell + 1):
                ks = range(shell + 1) if t == shell else [shell]
                part = sum(jnp.sum(products(k, t), axis=0, keepdims=True) for k in ks)
                for u in range(0, chunk, q):
                    cross_stage[(t * chunk + u) // q, 0:1, :] += part[:, u:u + q]

        @pl.when(place > 0)
        def _():
            onward.wait_recv()
            cross_stage[...] += passed[...]

        @pl.when(place < span - 1)
        def _():
            onward.start()

        @pl.when(place == span - 1)
        def _():
            cross_sends(lambda copy: copy.start())

    @pl.when(jnp.logical_not(above))
    def _():
        for shell in range(layers):
            side_operand(shell)
            across_operand(shell)
            for k in range(shell + 1):
                part = 0.0
                for t in range(shell + 1) if k == shell else [shell]:
                    product = products(k, t)
                    part = part + sum(product[:, u:u + q] for u in range(0, chunk, q))
                sums[k] = part if k == shell else sums[k] + part
        for k in range(layers):
            stage[k, 0:1, :] = jnp.sum(sums[k].T, axis=0, keepdims=True)
        plane_sends(lambda copy: copy.start(), lambda copy: copy.start())

    total[...] = jnp.zeros_like(total)

    def take(slot):
        pltpu.make_async_remote_copy(
            src_ref=stage.at[0], dst_ref=inbox.at[slot], send_sem=plane_send.at[0, 0], recv_sem=inbox_recv.at[slot],
            device_id=at(layer, row, col), device_id_type=MESH).wait_recv()
        total[...] += inbox[slot]

    for l in range(layers):
        for c in range(cols):
            here = jnp.logical_and(l == layer, c == col)

            @pl.when(jnp.logical_and(here, jnp.logical_not(above)))
            def _():
                to_self.wait()
                total[...] += inbox[l * cols + c]

            @pl.when(jnp.logical_and(jnp.logical_not(here), c <= group))
            def _():
                take(l * cols + c)
    for g in range(cols):
        @pl.when(g < group)
        def _():
            for l in range(layers):
                take(layers * cols + g * layers + l)

    part = q // cols
    mine = jnp.zeros((2, part), jnp.float32)
    for c in range(cols):
        mine = jnp.where(c == col, total[:, c * part:(c + 1) * part], mine)
    out_ref[...] = clustering_of(mine[0:1], mine[1:2]) if finish else mine

    across_sends(lambda copy: copy.wait_send())
    side_sends(lambda copy: copy.wait_send())

    @pl.when(jnp.logical_and(above, place < span - 1))
    def _():
        onward.wait_send()

    @pl.when(jnp.logical_and(above, place == span - 1))
    def _():
        cross_sends(lambda copy: copy.wait_send())

    @pl.when(jnp.logical_not(above))
    def _():
        plane_sends(lambda copy: copy.wait_send(), lambda copy: None)


def clustering_of(triangles, degree):
    return 2.0 * triangles / jnp.maximum(degree * (degree - 1.0), 2.0)


def two_blocks(edge_weight, finish):
    layers, rows, cols = (lax.axis_size(a) for a in ("layer", "row", "col"))
    m, n = edge_weight.shape
    q, span = m // layers, rows // cols
    slots = 2 * layers * cols
    dma, flag = pltpu.SemaphoreType.DMA, pltpu.SemaphoreType.REGULAR
    kind = edge_weight.dtype
    return pl.pallas_call(
        functools.partial(kernel, layers, rows, cols, finish),
        out_shape=jax.ShapeDtypeStruct((1 if finish else 2, q // cols), jnp.float32),
        in_specs=[pl.BlockSpec(memory_space=pl.ANY)],
        out_specs=pl.BlockSpec(memory_space=pltpu.VMEM),
        scratch_shapes=[
            pltpu.VMEM((m, n), kind),
            pltpu.VMEM((m, span * q), kind),
            pltpu.VMEM((span * q, n), kind),
            pltpu.VMEM((layers, q, q), jnp.float32),
            pltpu.VMEM((layers, 2, q), jnp.float32),
            pltpu.VMEM((span * layers, 2, q), jnp.float32),
            pltpu.VMEM((span * layers, 2, q), jnp.float32),
            pltpu.VMEM((2, q), jnp.float32),
            pltpu.VMEM((slots, 2, q), jnp.float32),
            dma, dma((span,)), dma, dma, dma((span, layers, cols)), dma((span, layers)),
            dma((span, layers)), dma((span, layers)), dma, dma, dma((layers, cols)), dma((span * layers, cols)), dma((slots,)),
            flag, flag,
        ],
        compiler_params=pltpu.CompilerParams(collective_id=0, has_side_effects=True),
    )(edge_weight)


def three_blocks(edge_weight):
    layers, layer_index = lax.axis_size("layer"), lax.axis_index("layer")
    row_count, col_count = edge_weight.shape
    row_block = (lax.axis_index("row") * row_count + jnp.arange(row_count, dtype=jnp.int32)) // col_count
    lower = jnp.where(row_block[:, None] > lax.axis_index("col"), edge_weight, jnp.zeros_like(edge_weight))
    column_groups = lower.reshape(row_count, col_count // (STRIPE * layers), layers, STRIPE)
    left_local = lax.dynamic_index_in_dim(column_groups, layer_index, 2, keepdims=False).reshape(
        row_count, col_count // layers
    )
    row_groups = lower.reshape(row_count // (STRIPE * layers), layers, STRIPE, col_count)
    right_local = lax.dynamic_index_in_dim(row_groups, layer_index, 1, keepdims=False).reshape(
        row_count // layers, col_count
    )
    left_whole = lax.all_gather(left_local, "col", axis=1, tiled=True)
    right_whole = lax.all_gather(right_local, "row", axis=0, tiled=True)
    paths = jnp.dot(left_whole, right_whole, preferred_element_type=jnp.float32)
    triangles = jnp.sum(paths * lower, axis=1)
    layer_share = lax.psum_scatter(triangles, "layer", scatter_dimension=0, tiled=True)
    return lax.psum_scatter(layer_share, "col", scatter_dimension=0, tiled=True)


def local(edge_weight):
    if lax.axis_size("col") == 2:
        return two_blocks(edge_weight, finish=True)
    triangles, degree = two_blocks(edge_weight, finish=False)
    return clustering_of(triangles + three_blocks(edge_weight), degree).reshape(1, -1)


def solution(mesh):
    placed = (P("row", "col"),)
    return jax.shard_map(
        local, mesh=mesh, in_specs=placed, out_specs=P("row", ("layer", "col")), check_vma=False
    )
```

```python
import functools

import jax
import jax.numpy as jnp
from jax import lax
from jax.experimental import pallas as pl
from jax.experimental.pallas import tpu as pltpu
from jax.sharding import PartitionSpec as P

STRIPE = 128
MESH = pl.DeviceIdType.MESH


def at(layer, row, col):
    return {"layer": layer, "row": row, "col": col}


def kernel(
    layers, rows, cols, finish, w_ref, out_ref,
    block, side, across, later_side, later_across, lend, lent, sums, stage, cross_stage, passed, total, inbox,
    load_sem, keep_side_sem, keep_across_sem, keep_inbox_sem, side_send, side_recv,
    across_send, across_recv, pass_send, pass_recv, lend_send, lend_recv, plane_send, cross_send, inbox_recv, plane_in, above_in,
):
    span = rows // cols
    m, n = w_ref.shape
    q = m // layers
    chunk = n // layers
    split = layers // 2
    layer, row, col = (lax.axis_index(a) for a in ("layer", "row", "col"))
    group = row // span
    place = row % span
    above = col > group
    diagonal = col == group
    share = jnp.where(layer % 2 == 0, layer // 2, layers - 1 - layer // 2)

    load = pltpu.make_async_copy(w_ref, block, load_sem)
    load.start()

    barrier = pltpu.get_barrier_semaphore()

    def greet(l, r, c, semaphore=barrier):
        pl.semaphore_signal(semaphore, inc=1, device_id=at(l, r, c), device_id_type=MESH)

    near = layers - 1 + cols - 1
    for c in range(cols):
        @pl.when(c != col)
        def _():
            greet(layer, row, c)
    for r in range(rows):
        is_near = jnp.logical_and(
            r != row, jnp.logical_or(r // span == group, jnp.logical_or(r == row - 1, r == row + 1)))
        near = near + jnp.where(is_near, 1, 0)

        @pl.when(is_near)
        def _():
            greet(layer, r, col)
    for l in range(layers):
        @pl.when(l != layer)
        def _():
            greet(l, row, col)

    def side_source(s, k):
        return w_ref.at[k * q:(k + 1) * q, pl.ds(pl.multiple_of(s * m + share * q, q), q)]

    def side_slot(s, k):
        return side.at[k * q:(k + 1) * q, s * q:(s + 1) * q]

    def across_source(t):
        return w_ref.at[pl.ds(pl.multiple_of(share * q, q), q), t * chunk:(t + 1) * chunk]

    def across_slot(s, t):
        return across.at[pl.ds(pl.multiple_of(s * q, q), q), t * chunk:(t + 1) * chunk]

    keep_across = pltpu.make_async_copy(
        w_ref.at[pl.ds(pl.multiple_of(share * q, q), q), :],
        across.at[pl.ds(pl.multiple_of(place * q, q), q), :], keep_across_sem)
    keep_across.start()

    def keep_side(s):
        return pltpu.make_async_copy(
            w_ref.at[:, pl.ds(pl.multiple_of(s * m + share * q, q), q)], side.at[:, s * q:(s + 1) * q],
            keep_side_sem.at[s])

    for s in range(span):
        @pl.when(s > place)
        def _():
            side[:, s * q:(s + 1) * q] = jnp.zeros((m, q), side.dtype)
            across[s * q:(s + 1) * q, :] = jnp.zeros((q, n), across.dtype)

        @pl.when(jnp.logical_and(s < place, jnp.logical_not(diagonal)))
        def _():
            across[s * q:(s + 1) * q, split * chunk:] = jnp.zeros((q, n - split * chunk), across.dtype)

        @pl.when(jnp.logical_and(diagonal, s <= place))
        def _():
            keep_side(s).start()

    pl.semaphore_wait(barrier, near)

    def side_copy(s, k, c, later=False):
        return pltpu.make_async_remote_copy(
            src_ref=side_source(s, k), dst_ref=(later_side.at[s, k * q:(k + 1) * q] if later else side_slot(s, k)), send_sem=side_send.at[s, k, c],
            recv_sem=side_recv.at[s, k], device_id=at(layer, row, c), device_id_type=MESH)

    def side_has_entries(s, k):
        return jnp.logical_or(s < place, jnp.logical_and(s == place, k >= share))

    def side_sends(act):
        for k in range(layers):
            for s in range(span):
                for c in range(cols):
                    @pl.when(jnp.logical_and(jnp.logical_and(diagonal, c != col), side_has_entries(s, k)))
                    def _():
                        act(side_copy(s, k, c))

                    @pl.when(jnp.logical_and(jnp.logical_and(diagonal, c != col), s > place))
                    def _():
                        act(side_copy(s, k, c, True))

    def across_copy(s, t, origin, later=False):
        return pltpu.make_async_remote_copy(
            src_ref=across_source(t), dst_ref=(later_across.at[origin, :, t * chunk:(t + 1) * chunk] if later else across_slot(origin, t)), send_sem=across_send.at[s, t],
            recv_sem=across_recv.at[origin, t], device_id=at(layer, group * span + s, col), device_id_type=MESH)

    def has_entries(origin, t):
        return jnp.where(diagonal, t * chunk < (origin + 1) * m, t < split)

    def across_sends(act):
        for t in range(layers):
            for s in range(span):
                @pl.when(jnp.logical_and(s > place, has_entries(place, t)))
                def _():
                    act(across_copy(s, t, place))

                if t >= split:
                    @pl.when(jnp.logical_and(s < place, jnp.logical_not(diagonal)))
                    def _():
                        act(across_copy(s, t, place, True))

    across_sends(lambda copy: copy.start())
    side_sends(lambda copy: copy.start())

    for c in range(cols):
        @pl.when(c != col)
        def _():
            greet(layer, row, c, plane_in)

    load.wait()
    per_layer = n // layers
    row_here = row * m + lax.broadcasted_iota(jnp.int32, (q, 1), 0)
    col_here = col * n + lax.broadcasted_iota(jnp.int32, (1, n), 1)

    @pl.when(diagonal)
    def _():
        for k in range(layers):
            held = block[k * q:(k + 1) * q, :].astype(jnp.float32)
            block[k * q:(k + 1) * q, :] = jnp.where(row_here + k * q > col_here, held, 0.0).astype(block.dtype)

    pl.semaphore_wait(plane_in, cols - 1)

    @pl.when(jnp.logical_and(row >= span - 1, row < rows - 1))
    def _():
        pl.semaphore_wait(above_in, 1)

    @pl.when(row > span - 1)
    def _():
        greet(layer, row - 1, col, above_in)

    @pl.when(jnp.logical_not(above))
    def _():
        mine = pl.ds(pl.multiple_of(layer * per_layer, per_layer), per_layer)
        for k in range(layers):
            linked = jnp.where(block[k * q:(k + 1) * q, mine].astype(jnp.float32) > 0, 1.0, 0.0)
            counts = sum(linked[:, t:t + q] for t in range(0, per_layer, q))
            stage[k, 1:2, :] = jnp.sum(counts.T, axis=0, keepdims=True)

    keep_across.wait()
    for s in range(span):
        @pl.when(jnp.logical_and(diagonal, s <= place))
        def _():
            keep_side(s).wait()

    def side_operand(k):
        for s in range(span):
            @pl.when(jnp.logical_and(jnp.logical_not(diagonal), side_has_entries(s, k)))
            def _():
                side_copy(s, k, 0).wait_recv()

            @pl.when(s == place)
            def _():
                inner = row * m + share * q + lax.broadcasted_iota(jnp.int32, (1, q), 1)
                held = side[k * q:(k + 1) * q, s * q:(s + 1) * q].astype(jnp.float32)
                side[k * q:(k + 1) * q, s * q:(s + 1) * q] = jnp.where(
                    row_here + k * q > inner, held, 0.0).astype(side.dtype)

    def across_operand(t):
        for s in range(span):
            @pl.when(jnp.logical_and(s < place, has_entries(s, t)))
            def _():
                across_copy(0, t, s).wait_recv()

            @pl.when(diagonal)
            def _():
                inner = (group * span + s) * m + share * q + lax.broadcasted_iota(jnp.int32, (q, 1), 0)
                outer = col * n + t * chunk + lax.broadcasted_iota(jnp.int32, (1, chunk), 1)
                held = across[s * q:(s + 1) * q, t * chunk:(t + 1) * chunk].astype(jnp.float32)
                across[s * q:(s + 1) * q, t * chunk:(t + 1) * chunk] = jnp.where(
                    inner > outer, held, 0.0).astype(across.dtype)

    def products(k, t):
        here = slice(t * chunk, (t + 1) * chunk)
        paths = jnp.dot(side[k * q:(k + 1) * q, :], across[:, here], preferred_element_type=jnp.float32)
        return paths * block[k * q:(k + 1) * q, here].astype(jnp.float32)

    def later_products(s, act):
        @pl.when(s > place)
        def _():
            for k in range(layers):
                side_copy(s, k, 0, True).wait_recv()
            for t in range(split, layers):
                across_copy(0, t, s, True).wait_recv()
                here = slice(t * chunk, (t + 1) * chunk)
                paths = lax.dot_general(
                    later_side[s], block[:, here], (((0,), (0,)), ((), ())), preferred_element_type=jnp.float32)
                act(t, paths * later_across[s, :, here].astype(jnp.float32))

    lending = lambda s: pltpu.make_async_remote_copy(
        src_ref=lend.at[s], dst_ref=lent.at[place], send_sem=lend_send.at[s], recv_sem=lend_recv.at[place],
        device_id=at(layer, group * span + s, col), device_id_type=MESH)

    in_plane = lambda l, c: pltpu.make_async_remote_copy(
        src_ref=stage.at[l], dst_ref=inbox.at[layer * cols + col], send_sem=plane_send.at[l, c],
        recv_sem=inbox_recv.at[layer * cols + col], device_id=at(l, row, c), device_id_type=MESH)
    to_self = pltpu.make_async_copy(stage.at[layer], inbox.at[layer * cols + col], keep_inbox_sem)

    def plane_sends(act, self_act):
        for l in range(layers):
            for c in range(cols):
                here = jnp.logical_and(l == layer, c == col)

                @pl.when(jnp.logical_not(here))
                def _():
                    act(in_plane(l, c))

                @pl.when(here)
                def _():
                    self_act(to_self)

    onward = pltpu.make_async_remote_copy(
        src_ref=cross_stage, dst_ref=passed, send_sem=pass_send, recv_sem=pass_recv,
        device_id=at(layer, jnp.minimum(row + 1, rows - 1), col), device_id_type=MESH)
    cross_slot = layers * cols + group * layers + layer
    cross = lambda s, l, c: pltpu.make_async_remote_copy(
        src_ref=cross_stage.at[s * layers + l], dst_ref=inbox.at[cross_slot],
        send_sem=cross_send.at[s * layers + l, c], recv_sem=inbox_recv.at[cross_slot],
        device_id=at(l, col * span + s, c), device_id_type=MESH)

    def cross_sends(act):
        for s in reversed(range(span)):
            for l in range(layers):
                for c in range(cols):
                    act(cross(s, l, c))

    @pl.when(above)
    def _():
        cross_stage[...] = jnp.zeros_like(cross_stage)
        for shell in range(layers):
            side_operand(shell)
            across_operand(shell)
            for t in range(shell + 1):
                ks = range(shell + 1) if t == shell else [shell]
                part = sum(jnp.sum(products(k, t), axis=0, keepdims=True) for k in ks)
                for u in range(0, chunk, q):
                    cross_stage[(t * chunk + u) // q, 0:1, :] += part[:, u:u + q]

        def add_columns(t, product):
            part = jnp.sum(product, axis=0, keepdims=True)
            for u in range(0, chunk, q):
                cross_stage[(t * chunk + u) // q, 0:1, :] += part[:, u:u + q]

        for s in range(span):
            later_products(s, add_columns)

        @pl.when(place > 0)
        def _():
            onward.wait_recv()
            cross_stage[...] += passed[...]

        @pl.when(place < span - 1)
        def _():
            onward.start()

        @pl.when(place == span - 1)
        def _():
            cross_sends(lambda copy: copy.start())

    @pl.when(jnp.logical_not(above))
    def _():
        for shell in range(layers):
            side_operand(shell)
            across_operand(shell)
            for k in range(shell + 1):
                part = 0.0
                for t in range(shell + 1) if k == shell else [shell]:
                    product = products(k, t)
                    part = part + sum(product[:, u:u + q] for u in range(0, chunk, q))
                sums[k] = part if k == shell else sums[k] + part
        for k in range(layers):
            stage[k, 0:1, :] = jnp.sum(sums[k].T, axis=0, keepdims=True)

        @pl.when(jnp.logical_not(diagonal))
        def _():
            for s in range(span):
                def add_rows(t, product):
                    part = sum(product[:, u:u + q] for u in range(0, chunk, q))
                    part = jnp.sum(part.T, axis=0, keepdims=True)
                    lend[s, 0:1, :] = part if t == split else lend[s, 0:1, :] + part

                later_products(s, add_rows)

                @pl.when(s > place)
                def _():
                    lend[s, 1:2, :] = jnp.zeros((1, q), jnp.float32)
                    lending(s).start()

                @pl.when(s < place)
                def _():
                    pltpu.make_async_remote_copy(
                        src_ref=lend.at[s], dst_ref=lent.at[s], send_sem=lend_send.at[s], recv_sem=lend_recv.at[s],
                        device_id=at(layer, row, col), device_id_type=MESH).wait_recv()
                    for k in range(layers):
                        @pl.when(share == k)
                        def _():
                            stage[k] += lent[s]

        plane_sends(lambda copy: copy.start(), lambda copy: copy.start())

    total[...] = jnp.zeros_like(total)

    def take(slot):
        pltpu.make_async_remote_copy(
            src_ref=stage.at[0], dst_ref=inbox.at[slot], send_sem=plane_send.at[0, 0], recv_sem=inbox_recv.at[slot],
            device_id=at(layer, row, col), device_id_type=MESH).wait_recv()
        total[...] += inbox[slot]

    for l in range(layers):
        for c in range(cols):
            here = jnp.logical_and(l == layer, c == col)

            @pl.when(jnp.logical_and(here, jnp.logical_not(above)))
            def _():
                to_self.wait()
                total[...] += inbox[l * cols + c]

            @pl.when(jnp.logical_and(jnp.logical_not(here), c <= group))
            def _():
                take(l * cols + c)
    for g in range(cols):
        @pl.when(g < group)
        def _():
            for l in range(layers):
                take(layers * cols + g * layers + l)

    part = q // cols
    mine = jnp.zeros((2, part), jnp.float32)
    for c in range(cols):
        mine = jnp.where(c == col, total[:, c * part:(c + 1) * part], mine)
    out_ref[...] = clustering_of(mine[0:1], mine[1:2]) if finish else mine

    across_sends(lambda copy: copy.wait_send())
    side_sends(lambda copy: copy.wait_send())

    @pl.when(jnp.logical_and(above, place < span - 1))
    def _():
        onward.wait_send()

    @pl.when(jnp.logical_and(above, place == span - 1))
    def _():
        cross_sends(lambda copy: copy.wait_send())

    @pl.when(jnp.logical_not(above))
    def _():
        plane_sends(lambda copy: copy.wait_send(), lambda copy: None)

    @pl.when(col < group)
    def _():
        for s in range(span):
            @pl.when(s > place)
            def _():
                lending(s).wait_send()


def clustering_of(triangles, degree):
    return 2.0 * triangles / jnp.maximum(degree * (degree - 1.0), 2.0)


def two_blocks(edge_weight, finish):
    layers, rows, cols = (lax.axis_size(a) for a in ("layer", "row", "col"))
    m, n = edge_weight.shape
    q, span = m // layers, rows // cols
    slots = 2 * layers * cols
    dma, flag = pltpu.SemaphoreType.DMA, pltpu.SemaphoreType.REGULAR
    kind = edge_weight.dtype
    return pl.pallas_call(
        functools.partial(kernel, layers, rows, cols, finish),
        out_shape=jax.ShapeDtypeStruct((1 if finish else 2, q // cols), jnp.float32),
        in_specs=[pl.BlockSpec(memory_space=pl.ANY)],
        out_specs=pl.BlockSpec(memory_space=pltpu.VMEM),
        scratch_shapes=[
            pltpu.VMEM((m, n), kind),
            pltpu.VMEM((m, span * q), kind),
            pltpu.VMEM((span * q, n), kind),
            pltpu.VMEM((span, m, q), kind),
            pltpu.VMEM((span, q, n), kind),
            pltpu.VMEM((span, 2, q), jnp.float32),
            pltpu.VMEM((span, 2, q), jnp.float32),
            pltpu.VMEM((layers, q, q), jnp.float32),
            pltpu.VMEM((layers, 2, q), jnp.float32),
            pltpu.VMEM((span * layers, 2, q), jnp.float32),
            pltpu.VMEM((span * layers, 2, q), jnp.float32),
            pltpu.VMEM((2, q), jnp.float32),
            pltpu.VMEM((slots, 2, q), jnp.float32),
            dma, dma((span,)), dma, dma, dma((span, layers, cols)), dma((span, layers)),
            dma((span, layers)), dma((span, layers)), dma, dma, dma((span,)), dma((span,)), dma((layers, cols)), dma((span * layers, cols)), dma((slots,)),
            flag, flag,
        ],
        compiler_params=pltpu.CompilerParams(collective_id=0, has_side_effects=True),
    )(edge_weight)


def three_blocks(edge_weight):
    layers, layer_index = lax.axis_size("layer"), lax.axis_index("layer")
    row_count, col_count = edge_weight.shape
    row_block = (lax.axis_index("row") * row_count + jnp.arange(row_count, dtype=jnp.int32)) // col_count
    lower = jnp.where(row_block[:, None] > lax.axis_index("col"), edge_weight, jnp.zeros_like(edge_weight))
    column_groups = lower.reshape(row_count, col_count // (STRIPE * layers), layers, STRIPE)
    left_local = lax.dynamic_index_in_dim(column_groups, layer_index, 2, keepdims=False).reshape(
        row_count, col_count // layers
    )
    row_groups = lower.reshape(row_count // (STRIPE * layers), layers, STRIPE, col_count)
    right_local = lax.dynamic_index_in_dim(row_groups, layer_index, 1, keepdims=False).reshape(
        row_count // layers, col_count
    )
    left_whole = lax.all_gather(left_local, "col", axis=1, tiled=True)
    right_whole = lax.all_gather(right_local, "row", axis=0, tiled=True)
    paths = jnp.dot(left_whole, right_whole, preferred_element_type=jnp.float32)
    triangles = jnp.sum(paths * lower, axis=1)
    layer_share = lax.psum_scatter(triangles, "layer", scatter_dimension=0, tiled=True)
    return lax.psum_scatter(layer_share, "col", scatter_dimension=0, tiled=True)


def local(edge_weight):
    if lax.axis_size("col") == 2:
        return two_blocks(edge_weight, finish=True)
    triangles, degree = two_blocks(edge_weight, finish=False)
    return clustering_of(triangles + three_blocks(edge_weight), degree).reshape(1, -1)


def solution(mesh):
    placed = (P("row", "col"),)
    return jax.shard_map(
        local, mesh=mesh, in_specs=placed, out_specs=P("row", ("layer", "col")), check_vma=False
    )
```

```python
import functools

import jax
import jax.numpy as jnp
from jax import lax
from jax.experimental import pallas as pl
from jax.experimental.pallas import tpu as pltpu
from jax.sharding import PartitionSpec as P

STRIPE = 128
MESH = pl.DeviceIdType.MESH


def at(layer, row, col):
    return {"layer": layer, "row": row, "col": col}


def kernel(
    layers, rows, cols, finish, w_ref, out_ref,
    block, side, across, sums, stage, cross_stage, passed, total, inbox,
    load_sem, keep_side_sem, keep_across_sem, keep_inbox_sem, side_send, side_recv,
    across_send, across_recv, pass_send, pass_recv, plane_send, cross_send, inbox_recv, plane_in, above_in,
):
    span = rows // cols
    m, n = w_ref.shape
    q = m // layers
    chunk = n // layers
    layer, row, col = (lax.axis_index(a) for a in ("layer", "row", "col"))
    group = row // span
    place = row % span
    above = col > group
    diagonal = col == group
    share = jnp.where(layer % 2 == 0, layer // 2, layers - 1 - layer // 2)

    load = pltpu.make_async_copy(w_ref, block, load_sem)
    load.start()

    barrier = pltpu.get_barrier_semaphore()

    def greet(l, r, c, semaphore=barrier):
        pl.semaphore_signal(semaphore, inc=1, device_id=at(l, r, c), device_id_type=MESH)

    near = layers - 1 + cols - 1
    for c in range(cols):
        @pl.when(c != col)
        def _():
            greet(layer, row, c)
    for r in range(rows):
        is_near = jnp.logical_and(
            r != row, jnp.logical_or(r // span == group, jnp.logical_or(r == row - 1, r == row + 1)))
        near = near + jnp.where(is_near, 1, 0)

        @pl.when(is_near)
        def _():
            greet(layer, r, col)
    for l in range(layers):
        @pl.when(l != layer)
        def _():
            greet(l, row, col)

    def side_source(s, k):
        return w_ref.at[k * q:(k + 1) * q, pl.ds(pl.multiple_of(s * m + share * q, q), q)]

    def side_slot(s, k):
        return side.at[k * q:(k + 1) * q, s * q:(s + 1) * q]

    def across_source(t):
        return w_ref.at[pl.ds(pl.multiple_of(share * q, q), q), t * chunk:(t + 1) * chunk]

    def across_slot(s, t):
        return across.at[pl.ds(pl.multiple_of(s * q, q), q), t * chunk:(t + 1) * chunk]

    keep_across = pltpu.make_async_copy(
        w_ref.at[pl.ds(pl.multiple_of(share * q, q), q), :],
        across.at[pl.ds(pl.multiple_of(place * q, q), q), :], keep_across_sem)
    keep_across.start()

    def keep_side(s):
        return pltpu.make_async_copy(
            w_ref.at[:, pl.ds(pl.multiple_of(s * m + share * q, q), q)], side.at[:, s * q:(s + 1) * q],
            keep_side_sem.at[s])

    for s in range(span):
        @pl.when(s > place)
        def _():
            side[:, s * q:(s + 1) * q] = jnp.zeros((m, q), side.dtype)
            across[s * q:(s + 1) * q, :] = jnp.zeros((q, n), across.dtype)

        @pl.when(jnp.logical_and(diagonal, s <= place))
        def _():
            keep_side(s).start()

    pl.semaphore_wait(barrier, near)

    def side_copy(s, k, c):
        return pltpu.make_async_remote_copy(
            src_ref=side_source(s, k), dst_ref=side_slot(s, k), send_sem=side_send.at[s, k, c],
            recv_sem=side_recv.at[s, k], device_id=at(layer, row, c), device_id_type=MESH)

    def side_has_entries(s, k):
        return jnp.logical_or(s < place, jnp.logical_and(s == place, k >= share))

    def side_sends(act):
        for k in range(layers):
            for s in range(span):
                for c in range(cols):
                    @pl.when(jnp.logical_and(jnp.logical_and(diagonal, c != col), side_has_entries(s, k)))
                    def _():
                        act(side_copy(s, k, c))

    def across_copy(s, t, origin):
        return pltpu.make_async_remote_copy(
            src_ref=across_source(t), dst_ref=across_slot(origin, t), send_sem=across_send.at[s, t],
            recv_sem=across_recv.at[origin, t], device_id=at(layer, group * span + s, col), device_id_type=MESH)

    def has_entries(origin, t):
        return jnp.logical_or(jnp.logical_not(diagonal), t * chunk < (origin + 1) * m)

    def across_sends(act):
        for t in range(layers):
            for s in range(span):
                @pl.when(jnp.logical_and(s > place, has_entries(place, t)))
                def _():
                    act(across_copy(s, t, place))

    across_sends(lambda copy: copy.start())
    side_sends(lambda copy: copy.start())

    for c in range(cols):
        @pl.when(c != col)
        def _():
            greet(layer, row, c, plane_in)

    load.wait()
    per_layer = n // layers
    row_here = row * m + lax.broadcasted_iota(jnp.int32, (q, 1), 0)
    col_here = col * n + lax.broadcasted_iota(jnp.int32, (1, n), 1)

    @pl.when(diagonal)
    def _():
        for k in range(layers):
            held = block[k * q:(k + 1) * q, :].astype(jnp.float32)
            block[k * q:(k + 1) * q, :] = jnp.where(row_here + k * q > col_here, held, 0.0).astype(block.dtype)

    pl.semaphore_wait(plane_in, cols - 1)

    @pl.when(jnp.logical_and(col > 0, jnp.logical_and(row >= span - 1, row < rows - 1)))
    def _():
        pl.semaphore_wait(above_in, 1)

    @pl.when(jnp.logical_and(col > 0, row > span - 1))
    def _():
        greet(layer, row - 1, col, above_in)

    @pl.when(jnp.logical_not(above))
    def _():
        mine = pl.ds(pl.multiple_of(layer * per_layer, per_layer), per_layer)
        for k in range(layers):
            linked = jnp.where(block[k * q:(k + 1) * q, mine].astype(jnp.float32) > 0, 1.0, 0.0)
            counts = sum(linked[:, t:t + q] for t in range(0, per_layer, q))
            stage[k, 1:2, :] = jnp.sum(counts.T, axis=0, keepdims=True)

    keep_across.wait()
    for s in range(span):
        @pl.when(jnp.logical_and(diagonal, s <= place))
        def _():
            keep_side(s).wait()

    def side_operand(k):
        for s in range(span):
            @pl.when(jnp.logical_and(jnp.logical_not(diagonal), side_has_entries(s, k)))
            def _():
                side_copy(s, k, 0).wait_recv()

            @pl.when(s == place)
            def _():
                inner = row * m + share * q + lax.broadcasted_iota(jnp.int32, (1, q), 1)
                held = side[k * q:(k + 1) * q, s * q:(s + 1) * q].astype(jnp.float32)
                side[k * q:(k + 1) * q, s * q:(s + 1) * q] = jnp.where(
                    row_here + k * q > inner, held, 0.0).astype(side.dtype)

    def across_operand(t):
        for s in range(span):
            @pl.when(jnp.logical_and(s < place, has_entries(s, t)))
            def _():
                across_copy(0, t, s).wait_recv()

            @pl.when(diagonal)
            def _():
                inner = (group * span + s) * m + share * q + lax.broadcasted_iota(jnp.int32, (q, 1), 0)
                outer = col * n + t * chunk + lax.broadcasted_iota(jnp.int32, (1, chunk), 1)
                held = across[s * q:(s + 1) * q, t * chunk:(t + 1) * chunk].astype(jnp.float32)
                across[s * q:(s + 1) * q, t * chunk:(t + 1) * chunk] = jnp.where(
                    inner > outer, held, 0.0).astype(across.dtype)

    def products(k, t):
        here = slice(t * chunk, (t + 1) * chunk)
        paths = jnp.dot(side[k * q:(k + 1) * q, :], across[:, here], preferred_element_type=jnp.float32)
        return paths * block[k * q:(k + 1) * q, here].astype(jnp.float32)

    in_plane = lambda l, c: pltpu.make_async_remote_copy(
        src_ref=stage.at[l], dst_ref=inbox.at[layer * cols + col], send_sem=plane_send.at[l, c],
        recv_sem=inbox_recv.at[layer * cols + col], device_id=at(l, row, c), device_id_type=MESH)
    to_self = pltpu.make_async_copy(stage.at[layer], inbox.at[layer * cols + col], keep_inbox_sem)

    def plane_sends(act, self_act):
        for l in range(layers):
            for c in range(cols):
                here = jnp.logical_and(l == layer, c == col)

                @pl.when(jnp.logical_not(here))
                def _():
                    act(in_plane(l, c))

                @pl.when(here)
                def _():
                    self_act(to_self)

    onward = pltpu.make_async_remote_copy(
        src_ref=cross_stage, dst_ref=passed, send_sem=pass_send, recv_sem=pass_recv,
        device_id=at(layer, jnp.minimum(row + 1, rows - 1), col), device_id_type=MESH)
    cross_slot = layers * cols + group * layers + layer
    cross = lambda s, l, c: pltpu.make_async_remote_copy(
        src_ref=cross_stage.at[s * layers + l], dst_ref=inbox.at[cross_slot],
        send_sem=cross_send.at[s * layers + l, c], recv_sem=inbox_recv.at[cross_slot],
        device_id=at(l, col * span + s, c), device_id_type=MESH)

    def cross_sends(act):
        for s in reversed(range(span)):
            for l in range(layers):
                for c in range(cols):
                    act(cross(s, l, c))

    @pl.when(above)
    def _():
        cross_stage[...] = jnp.zeros_like(cross_stage)
        for shell in range(layers):
            side_operand(shell)
            across_operand(shell)
            for t in range(shell + 1):
                ks = range(shell + 1) if t == shell else [shell]
                part = sum(jnp.sum(products(k, t), axis=0, keepdims=True) for k in ks)
                for u in range(0, chunk, q):
                    cross_stage[(t * chunk + u) // q, 0:1, :] += part[:, u:u + q]

        @pl.when(place > 0)
        def _():
            onward.wait_recv()
            cross_stage[...] += passed[...]

        @pl.when(place < span - 1)
        def _():
            onward.start()

        @pl.when(place == span - 1)
        def _():
            cross_sends(lambda copy: copy.start())

    @pl.when(jnp.logical_not(above))
    def _():
        for shell in range(layers):
            side_operand(shell)
            across_operand(shell)
            for k in range(shell + 1):
                part = 0.0
                for t in range(shell + 1) if k == shell else [shell]:
                    product = products(k, t)
                    part = part + sum(product[:, u:u + q] for u in range(0, chunk, q))
                sums[k] = part if k == shell else sums[k] + part
        for k in range(layers):
            stage[k, 0:1, :] = jnp.sum(sums[k].T, axis=0, keepdims=True)
        plane_sends(lambda copy: copy.start(), lambda copy: copy.start())

    total[...] = jnp.zeros_like(total)

    def take(slot):
        pltpu.make_async_remote_copy(
            src_ref=stage.at[0], dst_ref=inbox.at[slot], send_sem=plane_send.at[0, 0], recv_sem=inbox_recv.at[slot],
            device_id=at(layer, row, col), device_id_type=MESH).wait_recv()
        total[...] += inbox[slot]

    for l in range(layers):
        for c in range(cols):
            here = jnp.logical_and(l == layer, c == col)

            @pl.when(jnp.logical_and(here, jnp.logical_not(above)))
            def _():
                to_self.wait()
                total[...] += inbox[l * cols + c]

            @pl.when(jnp.logical_and(jnp.logical_not(here), c <= group))
            def _():
                take(l * cols + c)
    for g in range(cols):
        @pl.when(g < group)
        def _():
            for l in range(layers):
                take(layers * cols + g * layers + l)

    part = q // cols
    mine = jnp.zeros((2, part), jnp.float32)
    for c in range(cols):
        mine = jnp.where(c == col, total[:, c * part:(c + 1) * part], mine)
    out_ref[...] = clustering_of(mine[0:1], mine[1:2]) if finish else mine

    across_sends(lambda copy: copy.wait_send())
    side_sends(lambda copy: copy.wait_send())

    @pl.when(jnp.logical_and(above, place < span - 1))
    def _():
        onward.wait_send()

    @pl.when(jnp.logical_and(above, place == span - 1))
    def _():
        cross_sends(lambda copy: copy.wait_send())

    @pl.when(jnp.logical_not(above))
    def _():
        plane_sends(lambda copy: copy.wait_send(), lambda copy: None)


def clustering_of(triangles, degree):
    return 2.0 * triangles / jnp.maximum(degree * (degree - 1.0), 2.0)


def two_blocks(edge_weight, finish):
    layers, rows, cols = (lax.axis_size(a) for a in ("layer", "row", "col"))
    m, n = edge_weight.shape
    q, span = m // layers, rows // cols
    slots = 2 * layers * cols
    dma, flag = pltpu.SemaphoreType.DMA, pltpu.SemaphoreType.REGULAR
    kind = edge_weight.dtype
    return pl.pallas_call(
        functools.partial(kernel, layers, rows, cols, finish),
        out_shape=pltpu.VMEM((1 if finish else 2, q // cols), jnp.float32),
        in_specs=[pl.BlockSpec(memory_space=pl.ANY)],
        out_specs=pl.BlockSpec(memory_space=pltpu.VMEM),
        scratch_shapes=[
            pltpu.VMEM((m, n), kind),
            pltpu.VMEM((m, span * q), kind),
            pltpu.VMEM((span * q, n), kind),
            pltpu.VMEM((layers, q, q), jnp.float32),
            pltpu.VMEM((layers, 2, q), jnp.float32),
            pltpu.VMEM((span * layers, 2, q), jnp.float32),
            pltpu.VMEM((span * layers, 2, q), jnp.float32),
            pltpu.VMEM((2, q), jnp.float32),
            pltpu.VMEM((slots, 2, q), jnp.float32),
            dma, dma((span,)), dma, dma, dma((span, layers, cols)), dma((span, layers)),
            dma((span, layers)), dma((span, layers)), dma, dma, dma((layers, cols)), dma((span * layers, cols)), dma((slots,)),
            flag, flag,
        ],
        compiler_params=pltpu.CompilerParams(collective_id=0, has_side_effects=True),
    )(edge_weight)


def three_blocks(edge_weight):
    layers, layer_index = lax.axis_size("layer"), lax.axis_index("layer")
    row_count, col_count = edge_weight.shape
    row_block = (lax.axis_index("row") * row_count + jnp.arange(row_count, dtype=jnp.int32)) // col_count
    lower = jnp.where(row_block[:, None] > lax.axis_index("col"), edge_weight, jnp.zeros_like(edge_weight))
    column_groups = lower.reshape(row_count, col_count // (STRIPE * layers), layers, STRIPE)
    left_local = lax.dynamic_index_in_dim(column_groups, layer_index, 2, keepdims=False).reshape(
        row_count, col_count // layers
    )
    row_groups = lower.reshape(row_count // (STRIPE * layers), layers, STRIPE, col_count)
    right_local = lax.dynamic_index_in_dim(row_groups, layer_index, 1, keepdims=False).reshape(
        row_count // layers, col_count
    )
    left_whole = lax.all_gather(left_local, "col", axis=1, tiled=True)
    right_whole = lax.all_gather(right_local, "row", axis=0, tiled=True)
    paths = jnp.dot(left_whole, right_whole, preferred_element_type=jnp.float32)
    triangles = jnp.sum(paths * lower, axis=1)
    layer_share = lax.psum_scatter(triangles, "layer", scatter_dimension=0, tiled=True)
    return lax.psum_scatter(layer_share, "col", scatter_dimension=0, tiled=True)


def local(edge_weight):
    if lax.axis_size("col") == 2:
        return two_blocks(edge_weight, finish=True)
    triangles, degree = two_blocks(edge_weight, finish=False)
    return clustering_of(triangles + three_blocks(edge_weight), degree).reshape(1, -1)


def solution(mesh):
    placed = (P("row", "col"),)
    return jax.shard_map(
        local, mesh=mesh, in_specs=placed, out_specs=P("row", ("layer", "col")), check_vma=False
    )
```
